32 devices in a mesh: groups: 2 (over x), hit: 8 (over z, y), query: 2 (over core).
Axes of the slice: x: 2, y: 2, z: 4, core: 2. Of those that a mesh axis runs over, the one named last changes fastest.
Arguments:
- hits: bfloat16 [16384, 512], P(('groups', 'hit', 'query')), parts along dimension 0, may hold values from -24 to 24
- order: int32 [32, 512], P(('groups', 'hit', 'query')), parts along dimension 0, may hold values from 0 to 511, each once within a row
- valid: int32 [16384], P(('groups', 'hit', 'query')), parts along dimension 0, may hold values 0 or 1
- reach: int32 [16384], P(('groups', 'hit', 'query')), parts along dimension 0, may hold values from 128 to 512, as said below
- enc_wq: bfloat16 [512, 512], replicated, may hold values from -3 to 3
- enc_wk: bfloat16 [512, 512], replicated, may hold values from -1 to 1
- enc_wv: bfloat16 [512, 512], replicated, may hold values from -0.25 to 0.25
- enc_wo: bfloat16 [512, 512], replicated, may hold values from -0.25 to 0.25
- enc_gain1: float32 [512], replicated, may hold values from 0.5 to 1.5
- ffn_up: bfloat16 [512, 2048], replicated, may hold values from -0.25 to 0.25
- ffn_down: bfloat16 [2048, 512], replicated, may hold values from -0.125 to 0.125
- enc_gain2: float32 [512], replicated, may hold values from 0.5 to 1.5
- object_queries: bfloat16 [512, 512], P(('groups', 'hit', 'query')), parts along dimension 0, may hold values from -48 to 48
- dec_wq: bfloat16 [512, 512], replicated, may hold values from -8 to 8
- dec_wk: bfloat16 [512, 512], replicated, may hold values from -0.25 to 0.25
- dec_wv: bfloat16 [512, 512], replicated, may hold values from -0.25 to 0.25
- dec_wo: bfloat16 [512, 512], replicated, may hold values from -0.25 to 0.25
- dec_gain: float32 [512], replicated, may hold values from 0.5 to 1.5
- out_proj: bfloat16 [512, 512], replicated, may hold values from -0.25 to 0.25
Outputs:
- encoded: bfloat16 [16384, 512], P(('groups', 'hit', 'query')), parts along dimension 0
- decoded: bfloat16 [512, 512], P(('groups', 'hit', 'query')), parts along dimension 0
The draws below stay inside these ranges and needn't reach their ends.
There are 2 independent parts, one for each index of `groups`. The reference program is written for one: setup_inputs(seed, part) draws one part's arguments, and reference() takes and returns one part's arrays. A program takes and returns all parts, laid end to end along the dimension named above; an argument that names none is the same for every part. Nothing has to cross between parts.
Inputs may be any that keep to these rules, and one draw needn't show every extreme that they name: The first hit of every block of 512 arrival positions has reach 512.
All inputs are finite; a program needn't handle non-finite values. No bound on the sum of `valid` on one device may be relied on, other than what follows from the above.
Results may differ from the reference program's by a relative error of at most 0.035.
Values may be sent and summed in bfloat16 or wider, within the bound.
No kernel may reach another device: no remote copies, remote signals or barrier semaphores. Data moves between devices by JAX's collectives and lax.ppermute only.
A program may use at most 192 MiB of HBM per device.

```python
import math
import jax
import jax.numpy as jnp
from jax import lax

D = 512
HEADS = 8
FF = 2048
WINDOW = 512
HIT_DEV = 512
BLOCKS = 16
HITS = 8192
QUERIES = 256
N_QUERY = 2


def draw_hits(key, part):
    first = jax.random.fold_in(key, 11)
    tracks_per_block = 8
    block_count = HITS // HIT_DEV
    track_centres = jnp.clip(jax.random.normal(jax.random.fold_in(first, 4), (block_count * tracks_per_block, D), jnp.float32), -4.0, 4.0)
    track_ids = jax.random.randint(jax.random.fold_in(first, 5), (HITS,), 0, tracks_per_block, dtype=jnp.int32)
    centre_rows = jnp.arange(HITS, dtype=jnp.int32) // HIT_DEV * tracks_per_block + track_ids
    own_noise = jnp.clip(jax.random.normal(jax.random.fold_in(first, 1), (HITS, D), jnp.float32), -6.0, 6.0)
    base = 0.8 * track_centres[centre_rows] + 0.6 * own_noise
    return base.astype(jnp.bfloat16)


def draw_reach(key, part):
    first = jax.random.fold_in(key, 23)
    drawn = jax.random.randint(first, (HITS,), WINDOW // 4, WINDOW + 1, dtype=jnp.int32)
    head = jnp.arange(HITS, dtype=jnp.int32) % HIT_DEV == 0
    return jnp.where(head, WINDOW, drawn).astype(jnp.int32)


def encoder_pair(key):
    first = jax.random.fold_in(key, 37)
    wk = jnp.clip(jax.random.normal(jax.random.fold_in(first, 1), (D, D), jnp.float32), -4.0, 4.0) / math.sqrt(D)
    noise = jnp.clip(jax.random.normal(jax.random.fold_in(first, 2), (D, D), jnp.float32), -4.0, 4.0) / math.sqrt(D)
    wq = noise
    return (wq, wk)


def draw_enc_wq(key, part):
    return encoder_pair(key)[0].astype(jnp.bfloat16)


def draw_enc_wk(key, part):
    return encoder_pair(key)[1].astype(jnp.bfloat16)


def draw_object_queries(key, part):
    first = jax.random.fold_in(key, 41)
    base = jnp.clip(jax.random.normal(jax.random.fold_in(first, 1), (QUERIES, D), jnp.float32), -6.0, 6.0)
    base = base * 0.125
    return base.astype(jnp.bfloat16)


def draw_dec_wq(key, part):
    first = jax.random.fold_in(key, 53)
    base = jnp.clip(jax.random.normal(first, (D, D), jnp.float32), -4.0, 4.0) * (16.0 / math.sqrt(D))
    return base.astype(jnp.bfloat16)


def with_ends(result, stream_key, low, high):
    spot = [jax.random.randint(jax.random.fold_in(stream_key, axis), (), 0, length) for axis, length in enumerate(result.shape)]
    widest = result.shape.index(max(result.shape))
    beside = spot[:widest] + [(spot[widest] + 1) % result.shape[widest]] + spot[widest + 1:]
    return result.at[tuple(spot)].set(low).at[tuple(beside)].set(high)


def bell_draw(stream_key, extent, scale, limit, kind=jnp.bfloat16):
    values = scale * jax.random.normal(stream_key, extent, jnp.float32)
    return jnp.clip(values, min=-limit, max=limit).astype(kind)


def setup_inputs(seed: int = 0, part: int = 0) -> dict:
    streams_of = jax.random.split(jax.random.key(seed), 20)
    own_keys = jax.random.split(jax.random.fold_in(streams_of[19], part), 20)
    return {
        "hits": draw_hits(jax.random.fold_in(jax.random.fold_in(streams_of[19], part), 71), part),
        "order": jax.vmap(lambda own: jax.random.permutation(own, HIT_DEV))(jax.random.split(own_keys[1], BLOCKS)).reshape((BLOCKS, HIT_DEV)).astype(jnp.int32),
        "valid": with_ends((jax.random.randint(own_keys[2], (HITS,), 0, 4) < 3).astype(jnp.int32), jax.random.fold_in(own_keys[2], 1), 0, 1),
        "reach": draw_reach(jax.random.fold_in(jax.random.fold_in(streams_of[19], part), 71), part),
        "enc_wq": draw_enc_wq(jax.random.fold_in(streams_of[19], 71), part),
        "enc_wk": draw_enc_wk(jax.random.fold_in(streams_of[19], 71), part),
        "enc_wv": bell_draw(streams_of[6], (D, D), D ** -0.5, 0.25),
        "enc_wo": bell_draw(streams_of[7], (D, D), D ** -0.5, 0.25),
        "enc_gain1": jnp.clip(1.0 + 0.1 * jax.random.normal(streams_of[8], (D,), jnp.float32), 0.5, 1.5),
        "ffn_up": bell_draw(streams_of[9], (D, FF), D ** -0.5, 0.25),
        "ffn_down": bell_draw(streams_of[10], (FF, D), FF ** -0.5, 0.125),
        "enc_gain2": jnp.clip(1.0 + 0.1 * jax.random.normal(streams_of[11], (D,), jnp.float32), 0.5, 1.5),
        "object_queries": draw_object_queries(jax.random.fold_in(jax.random.fold_in(streams_of[19], part), 71), part),
        "dec_wq": draw_dec_wq(jax.random.fold_in(streams_of[19], 71), part),
        "dec_wk": bell_draw(streams_of[14], (D, D), D ** -0.5, 0.25),
        "dec_wv": bell_draw(streams_of[15], (D, D), D ** -0.5, 0.25),
        "dec_wo": bell_draw(streams_of[16], (D, D), D ** -0.5, 0.25),
        "dec_gain": jnp.clip(1.0 + 0.1 * jax.random.normal(streams_of[17], (D,), jnp.float32), 0.5, 1.5),
        "out_proj": bell_draw(streams_of[18], (D, D), D ** -0.5, 0.25),
    }


def project(rows, weight):
    return jnp.dot(rows, weight, preferred_element_type=jnp.float32).astype(jnp.bfloat16)

def rms_norm(values, gain):
    scale = lax.rsqrt(lax.optimization_barrier(jnp.mean(values * values, axis=-1, keepdims=True)) + 1e-05)
    return values * scale * gain.astype(jnp.float32)

def band_attention(queries, keys, values, key_valid, reach):
    count = queries.shape[0]
    span = keys.shape[0]
    margin = (span - count) // 2
    width = queries.shape[1] // HEADS
    query_heads = queries.reshape(count, HEADS, width).astype(jnp.float32)
    key_heads = keys.reshape(span, HEADS, width).astype(jnp.float32)
    value_heads = values.reshape(span, HEADS, width).astype(jnp.float32)
    scores = jnp.einsum('qhd,khd->hqk', query_heads, key_heads) * (1.0 / math.sqrt(width))
    offset = jnp.arange(span, dtype=jnp.int32)[None, :] - (jnp.arange(count, dtype=jnp.int32)[:, None] + margin)
    allowed = (jnp.abs(offset) <= reach[:, None]) & ((key_valid[None, :] > 0) | (offset == 0))
    scores = jnp.where(allowed[None], scores, -jnp.inf)
    peak = lax.optimization_barrier(jnp.max(scores, axis=2, keepdims=True))
    expo = jnp.where(allowed[None], jnp.exp(scores - peak), 0.0)
    probs = (expo / lax.optimization_barrier(jnp.sum(expo, axis=2, keepdims=True))).astype(jnp.bfloat16)
    context = jnp.einsum('hqk,khd->qhd', probs.astype(jnp.float32), value_heads)
    return context.reshape(count, HEADS * width).astype(jnp.bfloat16)

def encoder_tail(context, sorted_hits, enc_wo, enc_gain1, ffn_up, ffn_down, enc_gain2):
    attn_res = jnp.dot(context, enc_wo, preferred_element_type=jnp.float32) + sorted_hits.astype(jnp.float32)
    middle = rms_norm(attn_res, enc_gain1).astype(jnp.bfloat16)
    hidden = jax.nn.gelu(jnp.dot(middle, ffn_up, preferred_element_type=jnp.float32), approximate=True).astype(jnp.bfloat16)
    ffn_res = jnp.dot(hidden, ffn_down, preferred_element_type=jnp.float32) + middle.astype(jnp.float32)
    return rms_norm(ffn_res, enc_gain2).astype(jnp.bfloat16)

def span_partial(queries, keys, values):
    count = queries.shape[0]
    span = keys.shape[0]
    width = queries.shape[1] // HEADS
    query_heads = queries.reshape(count, HEADS, width).astype(jnp.float32)
    key_heads = keys.reshape(span, HEADS, width).astype(jnp.float32)
    value_heads = values.reshape(span, HEADS, width).astype(jnp.float32)
    scores = jnp.einsum('qhd,khd->qhk', query_heads, key_heads) * (1.0 / math.sqrt(width))
    peak = lax.optimization_barrier(jnp.max(scores, axis=2))
    expo = jnp.exp(scores - peak[:, :, None])
    total = lax.optimization_barrier(jnp.sum(expo, axis=2))
    weights = expo.astype(jnp.bfloat16)
    output = jnp.einsum('qhk,khd->qhd', weights.astype(jnp.float32), value_heads)
    return (peak, total, output.reshape(count, HEADS * width))

def reference(hits, order, valid, reach, enc_wq, enc_wk, enc_wv, enc_wo, enc_gain1, ffn_up, ffn_down, enc_gain2, object_queries, dec_wq, dec_wk, dec_wv, dec_wo, dec_gain, out_proj):
    nblocks = order.shape[0]
    per_block = order.shape[1]
    place = (jnp.arange(nblocks, dtype=jnp.int32)[:, None] * per_block + order.astype(jnp.int32)).reshape(-1)
    sorted_hits = hits[place]
    sorted_valid = valid[place]
    sorted_reach = reach[place]
    total_hits = sorted_hits.shape[0]
    queries = project(sorted_hits, enc_wq)
    keys = project(sorted_hits, enc_wk)
    values = project(sorted_hits, enc_wv)
    wide_keys = jnp.concatenate([keys[total_hits - WINDOW:], keys, keys[:WINDOW]], axis=0)
    wide_values = jnp.concatenate([values[total_hits - WINDOW:], values, values[:WINDOW]], axis=0)
    wide_valid = jnp.concatenate([sorted_valid[total_hits - WINDOW:], sorted_valid, sorted_valid[:WINDOW]], axis=0)
    block = 512 if per_block % 512 == 0 else per_block

    def attend(index):
        start = index * block
        return band_attention(lax.dynamic_slice_in_dim(queries, start, block, 0), lax.dynamic_slice_in_dim(wide_keys, start, block + 2 * WINDOW, 0), lax.dynamic_slice_in_dim(wide_values, start, block + 2 * WINDOW, 0), lax.dynamic_slice_in_dim(wide_valid, start, block + 2 * WINDOW, 0), lax.dynamic_slice_in_dim(sorted_reach, start, block, 0))
    context = lax.map(attend, jnp.arange(total_hits // block, dtype=jnp.int32)).reshape(total_hits, D)
    encoded = encoder_tail(context, sorted_hits, enc_wo, enc_gain1, ffn_up, ffn_down, enc_gain2)
    dec_queries = project(object_queries, dec_wq)
    dec_keys = project(encoded, dec_wk)
    dec_values = project(encoded, dec_wv)
    span = per_block * N_QUERY

    def one_span(index):
        start = index * span
        return span_partial(dec_queries, lax.dynamic_slice_in_dim(dec_keys, start, span, 0), lax.dynamic_slice_in_dim(dec_values, start, span, 0))
    peaks, totals, outputs = lax.map(one_span, jnp.arange(total_hits // span, dtype=jnp.int32))
    width = D // HEADS
    top = lax.optimization_barrier(jnp.max(peaks, axis=0))
    factor = jnp.exp(peaks - top[None])
    denom = lax.optimization_barrier(jnp.sum(totals * factor, axis=0))
    numer = lax.optimization_barrier(jnp.sum(outputs * jnp.repeat(factor, width, axis=2), axis=0))
    cross = (numer / jnp.repeat(denom, width, axis=1)).astype(jnp.bfloat16)
    dec_res = jnp.dot(cross, dec_wo, preferred_element_type=jnp.float32) + object_queries.astype(jnp.float32)
    normed = rms_norm(dec_res, dec_gain).astype(jnp.bfloat16)
    decoded = jnp.dot(normed, out_proj, preferred_element_type=jnp.float32).astype(jnp.bfloat16)
    return (encoded, decoded)
```

```python
import functools
import math

import jax
import jax.numpy as jnp
from jax import lax
from jax.experimental import pallas as pl
from jax.experimental.pallas import tpu as pltpu
from jax.sharding import PartitionSpec as P

HEADS = 8
LANES = 128
SUBLANES = 16
EPS = 1e-05
MASKED = -1e30
LOG2E = math.log2(math.e)
F32 = jnp.float32
BF16 = jnp.bfloat16
NN = (((1,), (0,)), ((), ()))
NT = (((1,), (1,)), ((), ()))


def dot(a, b, dims=NN):
    return lax.dot_general(a, b, dims, preferred_element_type=F32)


def rms(values, gain):
    scale = lax.rsqrt(jnp.mean(values * values, axis=-1, keepdims=True) + EPS)
    return values * scale * gain


def lane_of(shape):
    return lax.broadcasted_iota(jnp.int32, shape, len(shape) - 1)


def row_of(shape):
    return lax.broadcasted_iota(jnp.int32, shape, len(shape) - 2)


def sort_body(hits, order, valid, reach, payload, reach_out):
    count = hits.shape[0]
    wide = jnp.broadcast_to(order[...].astype(F32), (LANES, count))
    place = jnp.concatenate(
        [wide[:, c : c + LANES].T for c in range(0, count, LANES)], axis=0
    ).astype(jnp.int32)
    parts = []
    reaches = jnp.zeros((count, 1), F32)
    for c in range(0, count, LANES):
        hot = place == lane_of((count, LANES)) + c
        parts.append(jnp.where(hot, 1.0, 0.0).astype(BF16))
        reaches += jnp.sum(
            jnp.where(hot, reach[:, c : c + LANES].astype(F32), 0.0), axis=1, keepdims=True
        )
    moves = jnp.concatenate(parts, axis=1)
    payload[:count, :] = dot(moves, hits[...]).astype(BF16)
    flags = jnp.broadcast_to(valid[...].astype(F32), (SUBLANES, count)).astype(BF16)
    payload[count:, :] = dot(flags, moves, NT).astype(BF16)
    reach_out[...] = jnp.broadcast_to(reaches, (count, LANES))


def head_lanes(shape, head):
    lane = lane_of(shape)
    half = shape[-1] // 2
    return lane < half if head % 2 == 0 else lane >= half


def bias_tile(rows, cols, row0, col0, reach, valid, shift, own):
    offset = (lane_of((rows, cols)) + (col0 + shift)) - (row_of((rows, cols)) + row0)
    near = jnp.abs(offset).astype(F32) <= reach
    seen = valid > 0.5
    if own:
        seen = seen | (offset == 0)
    return jnp.where(near & seen, 0.0, MASKED)


def softmax_parts(scores):
    peak = functools.reduce(
        jnp.maximum, [jnp.max(s, axis=1, keepdims=True) for s in scores]
    )
    return peak, [jnp.exp2(s - peak).astype(BF16) for s in scores]


def pair_attend(query, blocks):
    outs, peaks = [], []
    for head in range(2):
        mine = jnp.where(head_lanes(query.shape, head), query, jnp.zeros_like(query))
        scores = []
        for keys, _, bias in blocks:
            s = dot(mine, keys, NT)
            scores.append(s if bias is None else s + bias)
        peak, weights = softmax_parts(scores)
        total = None
        for w, (_, values, _) in zip(weights, blocks):
            held = jnp.where(head_lanes(values.shape, head), values, jnp.ones_like(values))
            part = dot(w, held)
            total = part if total is None else total + part
        outs.append(total)
        peaks.append(peak)
    low = head_lanes(outs[0].shape, 0)
    output = jnp.where(low, outs[0], outs[1])
    total = pltpu.roll(jnp.where(low, outs[1], outs[0]), outs[0].shape[1] // 2, 1)
    return output, total, peaks


def local_body(
    side, own, other, reach, wq, wk, wv, q_out, out, total, peak, keys, values, bias
):
    count = reach.shape[0]
    tile = count // 2
    right = side[0] == 0
    hits = own[:count, :]
    scale = LOG2E / math.sqrt(hits.shape[1] // HEADS)
    q_out[...] = (dot(hits, wq[...]) * scale).astype(BF16)
    keys[:count, :] = dot(hits, wk[...]).astype(BF16)
    values[:count, :] = dot(hits, wv[...]).astype(BF16)
    next_hits = other[:count, :]
    keys[count:, :] = dot(next_hits, wk[...]).astype(BF16)
    values[count:, :] = dot(next_hits, wv[...]).astype(BF16)
    shift = jnp.where(right, count, -count)
    own_valid = own[count : count + 1, :].astype(F32)
    other_valid = other[count : count + 1, :].astype(F32)
    bias[:, :count] = bias_tile(count, count, 0, 0, reach[:, :1], own_valid, 0, True)
    bias[:, count:] = bias_tile(count, count, 0, 0, reach[:, :1], other_valid, shift, False)
    peak[...] = jnp.zeros_like(peak)

    heavy = pl.multiple_of(jnp.where(right, tile, 0), tile)
    light = pl.multiple_of(jnp.where(right, 0, tile), tile)

    def tile_of(start, cols, first, width):
        rows = pl.ds(start, tile)
        blocks = [(keys[:count, cols], values[:count, cols], bias[rows, :count])]
        if width == count:
            blocks.append((keys[count:, cols], values[count:, cols], bias[rows, count:]))
        else:
            part = pl.ds(pl.multiple_of(count + first, tile), width)
            half = jnp.where(right, bias[rows, count : count + tile], bias[rows, count + tile :])
            blocks.append((keys[part, cols], values[part, cols], half))
        return pair_attend(q_out[rows, cols], blocks)

    for pair in range(HEADS // 2):
        cols = slice(pair * LANES, (pair + 1) * LANES)
        for start, width in ((heavy, count), (light, tile)):
            rows = pl.ds(start, tile)
            o, t, p = tile_of(start, cols, light, width)
            out[rows, cols] = o
            total[rows, cols] = t
            lane = lane_of((tile, LANES))
            now = peak[rows, :]
            for head in range(2):
                now = jnp.where(lane == 2 * pair + head, p[head], now)
            peak[rows, :] = now


def rest_body(
    side, own, other, reach, query, out1, total1, peak1, wk, wv, wo, gain1, up, down, gain2,
    encoded, keys, values, bias, context,
):
    count = reach.shape[0]
    tile = count // 2
    right = side[0] == 1
    hits = other[:count, :]
    keys[...] = dot(hits, wk[...]).astype(BF16)
    values[...] = dot(hits, wv[...]).astype(BF16)
    shift = jnp.where(right, count, -count)
    valid = other[count : count + 1, :].astype(F32)
    bias[...] = bias_tile(count, count, 0, 0, reach[:, :1], valid, shift, False)
    heavy = pl.multiple_of(jnp.where(right, tile, 0), tile)
    light = pl.multiple_of(jnp.where(right, 0, tile), tile)
    for pair in range(HEADS // 2):
        cols = slice(pair * LANES, (pair + 1) * LANES)
        for start, width in ((heavy, count), (light, tile)):
            rows = pl.ds(start, tile)
            if width == count:
                block = (keys[:, cols], values[:, cols], bias[rows, :])
            else:
                part = pl.ds(light, tile)
                half = jnp.where(right, bias[rows, :tile], bias[rows, tile:])
                block = (keys[part, cols], values[part, cols], half)
            o, t, p = pair_attend(query[rows, cols], [block])
            low = head_lanes(o.shape, 0)
            before, after = [], []
            for head in range(2):
                col = 2 * pair + head
                old = peak1[rows, col : col + 1]
                top = jnp.maximum(old, p[head])
                before.append(jnp.exp2(old - top))
                after.append(jnp.exp2(p[head] - top))
            b = jnp.where(low, before[0], before[1])
            a = jnp.where(low, after[0], after[1])
            whole = total1[rows, cols] * b + t * a
            context[rows, cols] = ((out1[rows, cols] * b + o * a) / whole).astype(BF16)
    middle = rms(dot(context[...], wo[...]) + own[:count, :].astype(F32), gain1[...]).astype(BF16)
    width = hits.shape[1]
    total = middle.astype(F32)
    for c in range(0, up.shape[1], width):
        hidden = jax.nn.gelu(dot(middle, up[:, c : c + width]), approximate=True).astype(BF16)
        total += dot(hidden, down[c : c + width, :])
    encoded[...] = rms(total, gain2[...]).astype(BF16)


def split3(value):
    high = value.astype(BF16)
    left = value - high.astype(F32)
    mid = left.astype(BF16)
    return high, mid, (left - mid.astype(F32)).astype(BF16)


def decode_own_body(enc, queries, wq, wk, wv, dq, out, total, peak):
    scale = LOG2E / math.sqrt(enc.shape[1] // HEADS)
    dq[...] = (dot(queries[...], wq[...]) * scale).astype(BF16)
    keys = dot(enc[...], wk[...]).astype(BF16)
    values = dot(enc[...], wv[...]).astype(BF16)
    lane = lane_of(peak.shape)
    now = jnp.zeros(peak.shape, F32)
    for pair in range(HEADS // 2):
        cols = slice(pair * LANES, (pair + 1) * LANES)
        o, t, p = pair_attend(dq[:, cols], [(keys[:, cols], values[:, cols], None)])
        out[:, cols] = o
        total[:, cols] = t
        for head in range(2):
            now = jnp.where(lane == 2 * pair + head, p[head], now)
    peak[...] = now


def decode_other_body(enc, dq, out1, total1, peak1, wk, wv, payload):
    keys = dot(enc[...], wk[...]).astype(BF16)
    values = dot(enc[...], wv[...]).astype(BF16)
    width = enc.shape[1]
    lane = lane_of(peak1.shape)
    tops = jnp.zeros(peak1.shape, F32)
    sums = jnp.zeros(peak1.shape, F32)
    for pair in range(HEADS // 2):
        cols = slice(pair * LANES, (pair + 1) * LANES)
        o, t, p = pair_attend(dq[:, cols], [(keys[:, cols], values[:, cols], None)])
        low = head_lanes(o.shape, 0)
        before, after = [], []
        for head in range(2):
            col = 2 * pair + head
            old = peak1[:, col : col + 1]
            top = jnp.maximum(old, p[head])
            before.append(jnp.exp2(old - top))
            after.append(jnp.exp2(p[head] - top))
            tops = jnp.where(lane == col, top, tops)
        b = jnp.where(low, before[0], before[1])
        a = jnp.where(low, after[0], after[1])
        whole = total1[:, cols] * b + t * a
        payload[:, cols] = ((out1[:, cols] * b + o * a) / whole).astype(BF16)
        half = LANES // 2
        for head in range(2):
            sums = jnp.where(
                lane == 2 * pair + head, whole[:, head * half : head * half + 1], sums
            )
    pieces = split3(tops) + split3(sums)
    packed = jnp.zeros(peak1.shape, F32)
    for i, piece in enumerate(pieces):
        value = piece.astype(F32)
        moved = pltpu.roll(value, i * HEADS, 1) if i else value
        packed = jnp.where((lane >= i * HEADS) & (lane < (i + 1) * HEADS), moved, packed)
    payload[:, width:] = packed.astype(BF16)


def merge_body(parts, objects, wo, gain, proj, decoded):
    spans, owned, _ = parts.shape
    width = objects.shape[1]
    each = width // HEADS
    tops, sums = [], []
    for s in range(spans):
        extra = parts[s, :, width:].astype(F32)
        cut = [extra[:, i * HEADS : (i + 1) * HEADS] for i in range(6)]
        tops.append(cut[0] + cut[1] + cut[2])
        sums.append(cut[3] + cut[4] + cut[5])
    top = functools.reduce(jnp.maximum, tops)
    shares = [t * jnp.exp2(p - top) for t, p in zip(sums, tops)]
    denom = functools.reduce(jnp.add, shares)
    numer = jnp.zeros((owned, width), F32)
    half = LANES // 2
    for s in range(spans):
        share = shares[s] / denom
        spread = jnp.concatenate(
            [jnp.broadcast_to(share[:, h : h + 1], (owned, each)) for h in range(HEADS)], axis=1
        )
        numer += parts[s, :, :width].astype(F32) * spread
    cross = numer.astype(BF16)
    normed = rms(dot(cross, wo[...]) + objects[...].astype(F32), gain[...]).astype(BF16)
    decoded[...] = dot(normed, proj[...]).astype(BF16)


def scratch_call(body, outs, scratch, operands, flops, moved, name):
    vmem = pl.BlockSpec(memory_space=pltpu.VMEM)
    smem = pl.BlockSpec(memory_space=pltpu.SMEM)
    specs = [smem if x.ndim == 1 else vmem for x in operands]
    return pl.pallas_call(
        body,
        out_shape=outs,
        in_specs=specs,
        out_specs=[vmem] * len(outs),
        scratch_shapes=scratch,
        compiler_params=pltpu.CompilerParams(vmem_limit_bytes=60 * 1024 * 1024),
        cost_estimate=pl.CostEstimate(flops=flops, bytes_accessed=moved, transcendentals=0),
        name=name,
    )(*operands)


def shape(dims, dtype):
    return jax.ShapeDtypeStruct(dims, dtype)


def on_device(
    hits, order, valid, reach,
    enc_wq, enc_wk, enc_wv, enc_wo, enc_gain1, ffn_up, ffn_down, enc_gain2,
    object_queries, dec_wq, dec_wk, dec_wv, dec_wo, dec_gain, out_proj,
):
    count, width = hits.shape
    owned = object_queries.shape[0]
    spans = lax.axis_size("hit")
    ring = lax.axis_size(("hit", "query"))
    cube = 2 * count * width * width

    swap = [(i, i ^ 1) for i in range(ring)]
    beyond = [(i, (i + 1) % ring if i % 2 else (i - 1) % ring) for i in range(ring)]
    side = lax.axis_index("query").astype(jnp.int32).reshape(1)

    gathered = lax.all_to_all(
        jnp.broadcast_to(object_queries[None], (spans, owned, width)), "hit", 0, 0
    ).reshape(spans * owned, width)

    payload, reach_rows = scratch_call(
        sort_body,
        [shape((count + SUBLANES, width), BF16), shape((count, LANES), F32)],
        [],
        [hits, order, valid[None], reach[None]],
        cube,
        2 * count * width * 2,
        "sort_hits",
    )
    far = lax.ppermute(payload, ("hit", "query"), beyond)
    near = lax.ppermute(payload, ("hit", "query"), swap)
    query, out1, total1, peak1 = scratch_call(
        local_body,
        [
            shape((count, width), BF16),
            shape((count, width), F32),
            shape((count, width), F32),
            shape((count, LANES), F32),
        ],
        [
            pltpu.VMEM((2 * count, width), BF16),
            pltpu.VMEM((2 * count, width), BF16),
            pltpu.VMEM((count, 2 * count), F32),
        ],
        [side, payload, near, reach_rows, enc_wq, enc_wk, enc_wv],
        20 * cube,
        16 * count * width,
        "attend_chip",
    )
    (encoded,) = scratch_call(
        rest_body,
        [shape((count, width), BF16)],
        [
            pltpu.VMEM((count, width), BF16),
            pltpu.VMEM((count, width), BF16),
            pltpu.VMEM((count, count), F32),
            pltpu.VMEM((count, width), BF16),
        ],
        [
            side, payload, far, reach_rows, query, out1, total1, peak1,
            enc_wk, enc_wv, enc_wo, enc_gain1[None], ffn_up, ffn_down, enc_gain2[None],
        ],
        20 * cube,
        30 * count * width,
        "attend_far",
    )
    partner = lax.ppermute(encoded, ("hit", "query"), swap)
    rows = spans * owned
    dq, dout, dtotal, dpeak = scratch_call(
        decode_own_body,
        [
            shape((rows, width), BF16),
            shape((rows, width), F32),
            shape((rows, width), F32),
            shape((rows, LANES), F32),
        ],
        [],
        [encoded, gathered, dec_wq, dec_wk, dec_wv],
        4 * cube,
        8 * count * width,
        "decode_own",
    )
    (parts,) = scratch_call(
        decode_other_body,
        [shape((rows, width + LANES), BF16)],
        [],
        [partner, dq, dout, dtotal, dpeak, dec_wk, dec_wv],
        4 * cube,
        8 * count * width,
        "decode_other",
    )
    exchanged = lax.all_to_all(parts.reshape(spans, owned, width + LANES), "hit", 0, 0)
    (decoded,) = scratch_call(
        merge_body,
        [shape((owned, width), BF16)],
        [],
        [exchanged, object_queries, dec_wo, dec_gain[None], out_proj],
        4 * owned * width * width,
        4 * width * width,
        "merge_spans",
    )
    return (encoded, decoded)


def solution(mesh):
    split = P(("groups", "hit", "query"), None)
    flat = P(("groups", "hit", "query"))
    same = P()
    in_specs = (
        split, split, flat, flat,
        same, same, same, same, same, same, same, same,
        split,
        same, same, same, same, same, same,
    )
    return jax.shard_map(
        on_device, mesh=mesh, in_specs=in_specs, out_specs=(split, split), check_vma=False
    )
```

```python
import functools
import math

import jax
import jax.numpy as jnp
from jax import lax
from jax.experimental import pallas as pl
from jax.experimental.pallas import tpu as pltpu
from jax.sharding import PartitionSpec as P

HEADS = 8
LANES = 128
SUBLANES = 16
EPS = 1e-05
MASKED = -1e30
LOG2E = math.log2(math.e)
F32 = jnp.float32
BF16 = jnp.bfloat16
NN = (((1,), (0,)), ((), ()))
NT = (((1,), (1,)), ((), ()))


def dot(a, b, dims=NN):
    return lax.dot_general(a, b, dims, preferred_element_type=F32)


def rms(values, gain):
    scale = lax.rsqrt(jnp.mean(values * values, axis=-1, keepdims=True) + EPS)
    return values * scale * gain


def lane_of(shape):
    return lax.broadcasted_iota(jnp.int32, shape, len(shape) - 1)


def row_of(shape):
    return lax.broadcasted_iota(jnp.int32, shape, len(shape) - 2)


def sort_body(hits, order, valid, reach, payload, reach_out):
    count = hits.shape[0]
    wide = jnp.broadcast_to(order[...].astype(F32), (LANES, count))
    place = jnp.concatenate(
        [wide[:, c : c + LANES].T for c in range(0, count, LANES)], axis=0
    ).astype(jnp.int32)
    parts = []
    reaches = jnp.zeros((count, 1), F32)
    for c in range(0, count, LANES):
        hot = place == lane_of((count, LANES)) + c
        parts.append(jnp.where(hot, 1.0, 0.0).astype(BF16))
        reaches += jnp.sum(
            jnp.where(hot, reach[:, c : c + LANES].astype(F32), 0.0), axis=1, keepdims=True
        )
    moves = jnp.concatenate(parts, axis=1)
    payload[:count, :] = dot(moves, hits[...]).astype(BF16)
    flags = jnp.broadcast_to(valid[...].astype(F32), (SUBLANES, count)).astype(BF16)
    payload[count:, :] = dot(flags, moves, NT).astype(BF16)
    reach_out[...] = jnp.broadcast_to(reaches, (count, LANES))


def head_lanes(shape, head):
    lane = lane_of(shape)
    half = shape[-1] // 2
    return lane < half if head % 2 == 0 else lane >= half


def bias_tile(rows, cols, row0, col0, reach, valid, shift, own):
    offset = (lane_of((rows, cols)) + (col0 + shift)) - (row_of((rows, cols)) + row0)
    near = jnp.abs(offset).astype(F32) <= reach
    seen = valid > 0.5
    if own:
        seen = seen | (offset == 0)
    return jnp.where(near & seen, 0.0, MASKED)


def softmax_parts(scores):
    peak = functools.reduce(
        jnp.maximum, [jnp.max(s, axis=1, keepdims=True) for s in scores]
    )
    return peak, [jnp.exp2(s - peak).astype(BF16) for s in scores]


def pair_attend(query, blocks):
    outs, peaks = [], []
    for head in range(2):
        mine = jnp.where(head_lanes(query.shape, head), query, jnp.zeros_like(query))
        scores = []
        for keys, _, bias in blocks:
            s = dot(mine, keys, NT)
            scores.append(s if bias is None else s + bias)
        peak, weights = softmax_parts(scores)
        total = None
        for w, (_, values, _) in zip(weights, blocks):
            held = jnp.where(head_lanes(values.shape, head), values, jnp.ones_like(values))
            part = dot(w, held)
            total = part if total is None else total + part
        outs.append(total)
        peaks.append(peak)
    low = head_lanes(outs[0].shape, 0)
    output = jnp.where(low, outs[0], outs[1])
    total = pltpu.roll(jnp.where(low, outs[1], outs[0]), outs[0].shape[1] // 2, 1)
    return output, total, peaks


def local_body(
    side, own, other, reach, wq, wk, wv, q_out, out, total, peak, keys, values, bias
):
    count = reach.shape[0]
    tile = count // 2
    right = side[0] == 0
    hits = own[:count, :]
    scale = LOG2E / math.sqrt(hits.shape[1] // HEADS)
    q_out[...] = (dot(hits, wq[...]) * scale).astype(BF16)
    keys[:count, :] = dot(hits, wk[...]).astype(BF16)
    values[:count, :] = dot(hits, wv[...]).astype(BF16)
    next_hits = other[:count, :]
    keys[count:, :] = dot(next_hits, wk[...]).astype(BF16)
    values[count:, :] = dot(next_hits, wv[...]).astype(BF16)
    shift = jnp.where(right, count, -count)
    own_valid = own[count : count + 1, :].astype(F32)
    other_valid = other[count : count + 1, :].astype(F32)
    bias[:, :count] = bias_tile(count, count, 0, 0, reach[:, :1], own_valid, 0, True)
    bias[:, count:] = bias_tile(count, count, 0, 0, reach[:, :1], other_valid, shift, False)
    peak[...] = jnp.zeros_like(peak)

    heavy = pl.multiple_of(jnp.where(right, tile, 0), tile)
    light = pl.multiple_of(jnp.where(right, 0, tile), tile)

    def tile_of(start, cols, first, width):
        rows = pl.ds(start, tile)
        blocks = [(keys[:count, cols], values[:count, cols], bias[rows, :count])]
        if width == count:
            blocks.append((keys[count:, cols], values[count:, cols], bias[rows, count:]))
        else:
            part = pl.ds(pl.multiple_of(count + first, tile), width)
            half = jnp.where(right, bias[rows, count : count + tile], bias[rows, count + tile :])
            blocks.append((keys[part, cols], values[part, cols], half))
        return pair_attend(q_out[rows, cols], blocks)

    for pair in range(HEADS // 2):
        cols = slice(pair * LANES, (pair + 1) * LANES)
        for start, width in ((heavy, count), (light, tile)):
            rows = pl.ds(start, tile)
            o, t, p = tile_of(start, cols, light, width)
            out[rows, cols] = o
            total[rows, cols] = t
            lane = lane_of((tile, LANES))
            now = peak[rows, :]
            for head in range(2):
                now = jnp.where(lane == 2 * pair + head, p[head], now)
            peak[rows, :] = now


def rest_body(
    side, own, other, reach, query, out1, total1, peak1, wk, wv, wo, gain1, up, down, gain2, objects, dec_wq,
    encoded, dq, keys, values, bias, context,
):
    scale = LOG2E / math.sqrt(own.shape[1] // HEADS)
    dq[...] = (dot(objects[...], dec_wq[...]) * scale).astype(BF16)
    count = reach.shape[0]
    tile = count // 2
    right = side[0] == 1
    hits = other[:count, :]
    keys[...] = dot(hits, wk[...]).astype(BF16)
    values[...] = dot(hits, wv[...]).astype(BF16)
    shift = jnp.where(right, count, -count)
    valid = other[count : count + 1, :].astype(F32)
    bias[...] = bias_tile(count, count, 0, 0, reach[:, :1], valid, shift, False)
    heavy = pl.multiple_of(jnp.where(right, tile, 0), tile)
    light = pl.multiple_of(jnp.where(right, 0, tile), tile)
    for pair in range(HEADS // 2):
        cols = slice(pair * LANES, (pair + 1) * LANES)
        for start, width in ((heavy, count), (light, tile)):
            rows = pl.ds(start, tile)
            if width == count:
                block = (keys[:, cols], values[:, cols], bias[rows, :])
            else:
                part = pl.ds(light, tile)
                half = jnp.where(right, bias[rows, :tile], bias[rows, tile:])
                block = (keys[part, cols], values[part, cols], half)
            o, t, p = pair_attend(query[rows, cols], [block])
            low = head_lanes(o.shape, 0)
            before, after = [], []
            for head in range(2):
                col = 2 * pair + head
                old = peak1[rows, col : col + 1]
                top = jnp.maximum(old, p[head])
                before.append(jnp.exp2(old - top))
                after.append(jnp.exp2(p[head] - top))
            b = jnp.where(low, before[0], before[1])
            a = jnp.where(low, after[0], after[1])
            whole = total1[rows, cols] * b + t * a
            context[rows, cols] = ((out1[rows, cols] * b + o * a) / whole).astype(BF16)
    middle = rms(dot(context[...], wo[...]) + own[:count, :].astype(F32), gain1[...]).astype(BF16)
    width = hits.shape[1]
    total = middle.astype(F32)
    for c in range(0, up.shape[1], width):
        hidden = jax.nn.gelu(dot(middle, up[:, c : c + width]), approximate=True).astype(BF16)
        total += dot(hidden, down[c : c + width, :])
    encoded[...] = rms(total, gain2[...]).astype(BF16)


def split3(value):
    high = value.astype(BF16)
    left = value - high.astype(F32)
    mid = left.astype(BF16)
    return high, mid, (left - mid.astype(F32)).astype(BF16)


def decode_own_body(enc, dq, wk, wv, out, total, peak):
    keys = dot(enc[...], wk[...]).astype(BF16)
    values = dot(enc[...], wv[...]).astype(BF16)
    lane = lane_of(peak.shape)
    now = jnp.zeros(peak.shape, F32)
    for pair in range(HEADS // 2):
        cols = slice(pair * LANES, (pair + 1) * LANES)
        o, t, p = pair_attend(dq[:, cols], [(keys[:, cols], values[:, cols], None)])
        out[:, cols] = o
        total[:, cols] = t
        for head in range(2):
            now = jnp.where(lane == 2 * pair + head, p[head], now)
    peak[...] = now


def decode_other_body(enc, dq, out1, total1, peak1, wk, wv, payload):
    keys = dot(enc[...], wk[...]).astype(BF16)
    values = dot(enc[...], wv[...]).astype(BF16)
    width = enc.shape[1]
    lane = lane_of(peak1.shape)
    tops = jnp.zeros(peak1.shape, F32)
    sums = jnp.zeros(peak1.shape, F32)
    for pair in range(HEADS // 2):
        cols = slice(pair * LANES, (pair + 1) * LANES)
        o, t, p = pair_attend(dq[:, cols], [(keys[:, cols], values[:, cols], None)])
        low = head_lanes(o.shape, 0)
        before, after = [], []
        for head in range(2):
            col = 2 * pair + head
            old = peak1[:, col : col + 1]
            top = jnp.maximum(old, p[head])
            before.append(jnp.exp2(old - top))
            after.append(jnp.exp2(p[head] - top))
            tops = jnp.where(lane == col, top, tops)
        b = jnp.where(low, before[0], before[1])
        a = jnp.where(low, after[0], after[1])
        whole = total1[:, cols] * b + t * a
        payload[:, cols] = ((out1[:, cols] * b + o * a) / whole).astype(BF16)
        half = LANES // 2
        for head in range(2):
            sums = jnp.where(
                lane == 2 * pair + head, whole[:, head * half : head * half + 1], sums
            )
    pieces = split3(tops) + split3(sums)
    packed = jnp.zeros(peak1.shape, F32)
    for i, piece in enumerate(pieces):
        value = piece.astype(F32)
        moved = pltpu.roll(value, i * HEADS, 1) if i else value
        packed = jnp.where((lane >= i * HEADS) & (lane < (i + 1) * HEADS), moved, packed)
    payload[:, width:] = packed.astype(BF16)


def merge_body(parts, objects, wo, gain, proj, decoded):
    spans, owned, _ = parts.shape
    width = objects.shape[1]
    each = width // HEADS
    tops, sums = [], []
    for s in range(spans):
        extra = parts[s, :, width:].astype(F32)
        cut = [extra[:, i * HEADS : (i + 1) * HEADS] for i in range(6)]
        tops.append(cut[0] + cut[1] + cut[2])
        sums.append(cut[3] + cut[4] + cut[5])
    top = functools.reduce(jnp.maximum, tops)
    shares = [t * jnp.exp2(p - top) for t, p in zip(sums, tops)]
    denom = functools.reduce(jnp.add, shares)
    numer = jnp.zeros((owned, width), F32)
    half = LANES // 2
    for s in range(spans):
        share = shares[s] / denom
        spread = jnp.concatenate(
            [jnp.broadcast_to(share[:, h : h + 1], (owned, each)) for h in range(HEADS)], axis=1
        )
        numer += parts[s, :, :width].astype(F32) * spread
    cross = numer.astype(BF16)
    normed = rms(dot(cross, wo[...]) + objects[...].astype(F32), gain[...]).astype(BF16)
    decoded[...] = dot(normed, proj[...]).astype(BF16)


def scratch_call(body, outs, scratch, operands, flops, moved, name):
    vmem = pl.BlockSpec(memory_space=pltpu.VMEM)
    smem = pl.BlockSpec(memory_space=pltpu.SMEM)
    specs = [smem if x.ndim == 1 else vmem for x in operands]
    return pl.pallas_call(
        body,
        out_shape=outs,
        in_specs=specs,
        out_specs=[vmem] * len(outs),
        scratch_shapes=scratch,
        compiler_params=pltpu.CompilerParams(vmem_limit_bytes=24 * 1024 * 1024),
        cost_estimate=pl.CostEstimate(flops=flops, bytes_accessed=moved, transcendentals=0),
        name=name,
    )(*operands)


def shape(dims, dtype):
    return jax.ShapeDtypeStruct(dims, dtype)


def on_device(
    hits, order, valid, reach,
    enc_wq, enc_wk, enc_wv, enc_wo, enc_gain1, ffn_up, ffn_down, enc_gain2,
    object_queries, dec_wq, dec_wk, dec_wv, dec_wo, dec_gain, out_proj,
):
    count, width = hits.shape
    owned = object_queries.shape[0]
    spans = lax.axis_size("hit")
    ring = lax.axis_size(("hit", "query"))
    cube = 2 * count * width * width

    swap = [(i, i ^ 1) for i in range(ring)]
    beyond = [(i, (i + 1) % ring if i % 2 else (i - 1) % ring) for i in range(ring)]
    side = lax.axis_index("query").astype(jnp.int32).reshape(1)

    gathered = lax.all_to_all(
        jnp.broadcast_to(object_queries[None], (spans, owned, width)), "hit", 0, 0
    ).reshape(spans * owned, width)

    payload, reach_rows = scratch_call(
        sort_body,
        [shape((count + SUBLANES, width), BF16), shape((count, LANES), F32)],
        [],
        [hits, order, valid[None], reach[None]],
        cube,
        2 * count * width * 2,
        "sort_hits",
    )
    far = lax.ppermute(payload, ("hit", "query"), beyond)
    near = lax.ppermute(payload, ("hit", "query"), swap)
    query, out1, total1, peak1 = scratch_call(
        local_body,
        [
            shape((count, width), BF16),
            shape((count, width), F32),
            shape((count, width), F32),
            shape((count, LANES), F32),
        ],
        [
            pltpu.VMEM((2 * count, width), BF16),
            pltpu.VMEM((2 * count, width), BF16),
            pltpu.VMEM((count, 2 * count), F32),
        ],
        [side, payload, near, reach_rows, enc_wq, enc_wk, enc_wv],
        20 * cube,
        16 * count * width,
        "attend_chip",
    )
    rows = spans * owned
    encoded, dq = scratch_call(
        rest_body,
        [shape((count, width), BF16), shape((rows, width), BF16)],
        [
            pltpu.VMEM((count, width), BF16),
            pltpu.VMEM((count, width), BF16),
            pltpu.VMEM((count, count), F32),
            pltpu.VMEM((count, width), BF16),
        ],
        [
            side, payload, far, reach_rows, query, out1, total1, peak1,
            enc_wk, enc_wv, enc_wo, enc_gain1[None], ffn_up, ffn_down, enc_gain2[None],
            gathered, dec_wq,
        ],
        20 * cube,
        30 * count * width,
        "attend_far",
    )
    partner = lax.ppermute(encoded, ("hit", "query"), swap)
    dout, dtotal, dpeak = scratch_call(
        decode_own_body,
        [
            shape((rows, width), F32),
            shape((rows, width), F32),
            shape((rows, LANES), F32),
        ],
        [],
        [encoded, dq, dec_wk, dec_wv],
        4 * cube,
        8 * count * width,
        "decode_own",
    )
    (parts,) = scratch_call(
        decode_other_body,
        [shape((rows, width + LANES), BF16)],
        [],
        [partner, dq, dout, dtotal, dpeak, dec_wk, dec_wv],
        4 * cube,
        8 * count * width,
        "decode_other",
    )
    exchanged = lax.all_to_all(parts.reshape(spans, owned, width + LANES), "hit", 0, 0)
    (decoded,) = scratch_call(
        merge_body,
        [shape((owned, width), BF16)],
        [],
        [exchanged, object_queries, dec_wo, dec_gain[None], out_proj],
        4 * owned * width * width,
        4 * width * width,
        "merge_spans",
    )
    return (encoded, decoded)


def solution(mesh):
    split = P(("groups", "hit", "query"), None)
    flat = P(("groups", "hit", "query"))
    same = P()
    in_specs = (
        split, split, flat, flat,
        same, same, same, same, same, same, same, same,
        split,
        same, same, same, same, same, same,
    )
    return jax.shard_map(
        on_device, mesh=mesh, in_specs=in_specs, out_specs=(split, split), check_vma=False
    )
```
